32 devices in a mesh: group: 2 (over x), space: 16 (over z, y, core).
Axes of the slice: x: 2, y: 2, z: 4, core: 2. Of those that a mesh axis runs over, the one named last changes fastest.
Arguments:
- images: float32 [4, 128, 128, 128], P('group', 'space'), parts along dimension 0, may hold values from -2.7 to 2.7
- weights: float32 [4, 2], P('group'), parts along dimension 0, may hold values from 0 to 1
Outputs:
- relaxed: float32 [4, 128, 128, 128], P('group', 'space'), parts along dimension 0
- spacing: float32 [4, 1], P('group'), parts along dimension 0
The draws below stay inside these ranges and needn't reach their ends.
There are 2 independent parts, one for each index of `group`. The reference program is written for one: setup_inputs(seed, part) draws one part's arguments, and reference() takes and returns one part's arrays. A program takes and returns all parts, laid end to end along the dimension named above; each array names one. Nothing has to cross between parts.
All inputs are finite; a program needn't handle non-finite values.
Results may differ from the reference program's by a relative error of at most 0.0002.
Values sent between devices are 32-bit elements; how exact they have to be, the bound alone decides.
No kernel may reach another device: no remote copies, remote signals or barrier semaphores. Data moves between devices by JAX's collectives and lax.ppermute only.
A program may use at most 64 MiB of HBM per device.

```python
import math
import jax
import jax.numpy as jnp
from jax import lax

LX = 128
LY = 128
LZ = 128
IMAGES = 2
ITERS = 2


def correlated_rows(noise):
    total = noise
    for offset in range(1, 16):
        total = total + jnp.roll(noise, offset, axis=1)
    return total * 0.25


def draw_images(key, part):
    extent = (IMAGES, LX, LY, LZ)
    first_key = jax.random.fold_in(key, 0)
    third_key = jax.random.fold_in(key, 2)
    ramp = jnp.arange(LX, dtype=jnp.float32) / (LX - 1)
    amplitude = (0.3 * jnp.exp(ramp * math.log(3.0)))[None, :, None, None]
    parity = (jnp.arange(LX, dtype=jnp.int32) % 2).astype(jnp.float32)
    alternation = (1.0 - 2.0 * parity)[None, :, None, None]
    coherent = jax.random.truncated_normal(first_key, -3.0, 3.0, extent, jnp.float32)
    white_noise = jax.random.truncated_normal(third_key, -3.0, 3.0, extent, jnp.float32)
    rough_part = jnp.clip(alternation * (0.85 * correlated_rows(coherent)) + 0.5 * white_noise, -3.0, 3.0)
    return amplitude * rough_part


def draw_weights(key, part):
    fractions = jax.random.uniform(key, (IMAGES,), jnp.float32, 0.1, 0.9)
    active = (jnp.arange(IMAGES, dtype=jnp.int32) < IMAGES - 1).astype(jnp.float32)
    fractions = fractions * active
    diagonal = jnp.eye(IMAGES, dtype=jnp.float32) * (1.0 - fractions)[:, None]
    upper = jnp.eye(IMAGES, k=1, dtype=jnp.float32) * fractions[:, None]
    return diagonal + upper


def setup_inputs(seed: int = 0, part: int = 0) -> dict:
    arg_keys = jax.random.split(jax.random.key(seed), 3)
    part_splits = jax.random.split(jax.random.fold_in(arg_keys[2], part), 3)
    return {
        "images": draw_images(jax.random.fold_in(jax.random.fold_in(arg_keys[2], part), 71), part),
        "weights": draw_weights(jax.random.fold_in(jax.random.fold_in(arg_keys[2], part), 71), part),
    }


time_step = 0.1
gradient_weight = 1.0


def wave_squares(length):
    indices = jnp.arange(length, dtype=jnp.int32)
    signed = jnp.where(indices <= length // 2, indices, indices - length)
    number = signed.astype(jnp.float32) * (2.0 * math.pi / length)
    return number * number


def reference(images, weights):
    squares = wave_squares(LX)[:, None, None] + wave_squares(LY)[None, :, None] + wave_squares(LZ)[None, None, :]
    damping = 1.0 / (1.0 + time_step * gradient_weight * squares * squares)
    coupling = time_step * squares * damping
    cell_count = LX * LY * LZ
    concentration = images
    spacings = []
    for iteration in range(ITERS):
        potential = concentration * concentration * concentration - concentration
        spectrum = jnp.fft.fftn(concentration, axes=(1, 2, 3)) * damping - jnp.fft.fftn(potential, axes=(1, 2, 3)) * coupling
        concentration = jnp.real(jnp.fft.ifftn(spectrum, axes=(1, 2, 3))).astype(jnp.float32)
        difference = concentration[1:] - concentration[:-1]
        spacings.append(jnp.sum(difference * difference, axis=(1, 2, 3)) / cell_count)
        concentration = jnp.einsum('ij,jxyz->ixyz', weights, concentration, precision=lax.Precision.HIGHEST)
    return concentration, jnp.stack(spacings)
```

```python
import math

import jax
import jax.numpy as jnp
import numpy as np
from jax import lax
from jax.sharding import PartitionSpec as P

ITERS = 2

high = lax.Precision.HIGH
time_step = 0.1
gradient_weight = 1.0


def basis(length):
    index = np.arange(length)
    frequency = np.minimum(index, length - index)
    angles = (frequency[:, None] * index[None, :] % length) * (2.0 * math.pi / length)
    rows = np.where((index <= length // 2)[:, None], np.cos(angles), np.sin(angles))
    single = (frequency == 0) | (2 * frequency == length)
    scale = np.where(single, math.sqrt(1.0 / length), math.sqrt(2.0 / length))
    return (rows * scale[:, None]).astype(np.float32)


def wave_squares(length, indices):
    signed = jnp.where(indices <= length // 2, indices, indices - length)
    number = signed.astype(jnp.float32) * (2.0 * math.pi / length)
    return number * number


def local(images, weights):
    image_count, first_local, second_length, third_length = images.shape
    space_size = lax.axis_size("space")
    position = lax.axis_index("space")
    first_length = first_local * space_size
    second_local = second_length // space_size
    first = jnp.asarray(basis(first_length)).reshape(first_length, space_size, first_local)
    second = jnp.asarray(basis(second_length)).reshape(space_size, second_local, second_length)
    third = jnp.asarray(basis(third_length))
    local_rows = position * second_local + jnp.arange(second_local, dtype=jnp.int32)
    squares = (
        wave_squares(second_length, local_rows)[:, None, None]
        + wave_squares(first_length, jnp.arange(first_length, dtype=jnp.int32))[None, :, None]
        + wave_squares(third_length, jnp.arange(third_length, dtype=jnp.int32))[None, None, :]
    )
    damping = 1.0 / (1.0 + time_step * gradient_weight * squares * squares)
    coupling = time_step * squares * damping
    cell_count = first_length * second_length * third_length

    def forward(values):
        values = jnp.einsum("sby,fxyz->fxsbz", second, values, precision=high)
        values = jnp.einsum("fxsbz,kz->sfbxk", values, third, precision=high)
        values = lax.all_to_all(values, "space", 0, 0, tiled=True)
        return jnp.einsum("asx,sfbxk->fbak", first, values, precision=high)

    def backward(values, extra):
        values = jnp.einsum("asx,fbak->sfbxk", first, values, precision=high)
        sent = values.reshape(space_size, -1, third_length)
        if extra is not None:
            rows = jnp.broadcast_to(extra, (space_size,) + extra.shape)
            sent = jnp.concatenate([sent, rows], 1)
        sent = lax.all_to_all(sent, "space", 0, 0, tiled=True)
        count = values.size // (space_size * third_length)
        received = sent[:, :count].reshape(values.shape)
        values = jnp.einsum("sfbxk,kz->fxsbz", received, third, precision=high)
        values = jnp.einsum("sby,fxsbz->fxyz", second, values, precision=high)
        return values, sent[:, count:]

    concentration = images
    spectrum = None
    sums = []
    for iteration in range(ITERS):
        potential = concentration * concentration * concentration - concentration
        if iteration == 0:
            spectra = forward(jnp.concatenate([concentration, potential]))
            spectrum, potential = spectra[:image_count], spectra[image_count:]
        else:
            potential = forward(potential)
        spectrum = spectrum * damping - potential * coupling
        difference = spectrum[1:] - spectrum[:-1]
        sums.append(jnp.sum(difference * difference, axis=(1, 2, 3)))
        spectrum = jnp.einsum("ij,jbak->ibak", weights, spectrum, precision=lax.Precision.HIGHEST)
        extra = None
        if iteration == ITERS - 1:
            partial_sums = jnp.concatenate(sums)
            extra = jnp.pad(partial_sums[None], ((0, 7), (0, third_length - partial_sums.size)))
        concentration, extra = backward(spectrum, extra)
    totals = jnp.sum(extra[:, 0], axis=0)[: ITERS * (image_count - 1)] / cell_count
    return (concentration, totals.reshape(ITERS, image_count - 1))


def solution(mesh):
    placed = (P("group", "space", None, None), P("group", None))
    return jax.shard_map(
        local,
        mesh=mesh,
        in_specs=placed,
        out_specs=(P("group", "space", None, None), P("group", None)),
        check_vma=False,
    )
```

```python
import functools
import math

import jax
import jax.numpy as jnp
import numpy as np
from jax import lax
from jax.experimental import pallas as pl
from jax.experimental.pallas import tpu as pltpu
from jax.sharding import PartitionSpec as P

ITERS = 2

high = lax.Precision.HIGH
time_step = 0.1
gradient_weight = 1.0


def basis(length):
    index = np.arange(length)
    frequency = np.minimum(index, length - index)
    angles = (frequency[:, None] * index[None, :] % length) * (2.0 * math.pi / length)
    rows = np.where((index <= length // 2)[:, None], np.cos(angles), np.sin(angles))
    single = (frequency == 0) | (2 * frequency == length)
    scale = np.where(single, math.sqrt(1.0 / length), math.sqrt(2.0 / length))
    return (rows * scale[:, None]).astype(np.float32)


def wave_squares(length, indices):
    signed = jnp.where(indices <= length // 2, indices, indices - length)
    number = signed.astype(jnp.float32) * (2.0 * math.pi / length)
    return number * number


def parts(matrix):
    upper = matrix.astype(jnp.bfloat16)
    return upper, (matrix - upper.astype(np.float32)).astype(jnp.bfloat16)


def left_table(matrix):
    upper, lower = parts(matrix)
    return np.concatenate([upper, upper, lower], 1)


def right_table(matrix):
    upper, lower = parts(matrix)
    return np.concatenate([upper, upper, lower], 0)


def split(values):
    upper = values.astype(jnp.bfloat16)
    lower = (values - upper.astype(jnp.float32)).astype(jnp.bfloat16)
    return upper, lower


def from_left(table, values):
    upper, lower = split(values)
    return jnp.dot(table, jnp.concatenate([upper, lower, upper], 0), preferred_element_type=jnp.float32)


def from_right(values, table):
    upper, lower = split(values)
    return jnp.dot(jnp.concatenate([upper, lower, upper], 1), table, preferred_element_type=jnp.float32)


def potential_of(values):
    return values * values * values - values


def enter_spectrum(sizes, planes, second_table, third_table, scratch, send):
    fields, space_size, first_local, second_local, second_length, third_length = sizes
    for x in range(first_local):
        mixed = from_left(second_table, planes(x))
        for f in range(fields):
            scratch[f, pl.ds(x * second_length, second_length), :] = mixed[:, f * third_length : (f + 1) * third_length]
    count = second_local * first_local
    for f in range(fields):
        for d in range(space_size):
            rows = [
                scratch[f, pl.ds(d * second_local + b, first_local, stride=second_length), :]
                for b in range(second_local)
            ]
            send[d, pl.ds(f * count, count), :] = from_right(jnp.concatenate(rows, 0), third_table)


def leave_spectrum(sizes, received, third_table, second_table, scratch, put):
    fields, space_size, first_local, second_local, second_length, third_length = sizes
    count = second_local * first_local
    for s in range(space_size):
        scratch[pl.ds(s * fields * count, fields * count), :] = from_right(
            received[s, pl.ds(0, fields * count), :], third_table
        )
    for x in range(first_local):
        columns = []
        for f in range(fields):
            rows = [
                scratch[pl.ds((s * fields + f) * count + x, second_local, stride=first_local), :]
                for s in range(space_size)
            ]
            columns.append(jnp.concatenate(rows, 0))
        put(x, from_left(second_table, jnp.concatenate(columns, 1)))


def enter_kernel(sizes, images, second_table, third_table, send, scratch):
    image_count = images.shape[0]

    def planes(x):
        values = jnp.concatenate([images[j, x] for j in range(image_count)], 1)
        return jnp.concatenate([values, potential_of(values)], 1)

    enter_spectrum(sizes, planes, second_table[...], third_table[...], scratch, send)


def relax_kernel(sizes, first, last, refs):
    image_count, space_size, first_local, second_local, second_length, third_length = sizes
    if first:
        weights, received, first_table, back_table, send, spectrum_out, sums_out = refs
        fields = 2 * image_count
    else:
        weights, received, spectrum_in, sums_in, first_table, back_table, send = refs[:7]
        if not last:
            spectrum_out, sums_out = refs[7:]
        fields = image_count
    first_length = space_size * first_local
    count = second_local * first_local
    position = lax.axis_index("space")
    shape = (first_length, third_length)
    across = wave_squares(first_length, lax.broadcasted_iota(jnp.int32, shape, 0)) + wave_squares(
        third_length, lax.broadcasted_iota(jnp.int32, shape, 1)
    )
    sums = [jnp.zeros((8, third_length), jnp.float32) for _ in range(image_count - 1)]
    forward = first_table[...]
    back = back_table[...]
    for b in range(second_local):
        columns = [
            received[:, pl.ds(f * count + b * first_local, first_local), :].reshape(first_length, third_length)
            for f in range(fields)
        ]
        spectra = from_left(forward, jnp.concatenate(columns, 1))
        spectra = [spectra[:, f * third_length : (f + 1) * third_length] for f in range(fields)]
        row = jnp.full((1, 1), position * second_local + b, jnp.int32)
        squares = across + wave_squares(second_length, row)
        damping = 1.0 / (1.0 + time_step * gradient_weight * squares * squares)
        coupling = time_step * squares * damping
        relaxed = []
        for j in range(image_count):
            field = spectra[j] if first else spectrum_in[b, j]
            potential = spectra[image_count + j] if first else spectra[j]
            relaxed.append(damping * field - coupling * potential)
        for j in range(image_count - 1):
            difference = relaxed[j + 1] - relaxed[j]
            sums[j] = sums[j] + jnp.sum((difference * difference).reshape(-1, 8, third_length), axis=0)
        mixed = []
        for i in range(image_count):
            total = weights[i, 0] * relaxed[0]
            for j in range(1, image_count):
                total = total + weights[i, j] * relaxed[j]
            if not last:
                spectrum_out[b, i] = total
            mixed.append(total)
        values = from_left(back, jnp.concatenate(mixed, 1))
        for j in range(image_count):
            send[:, pl.ds(j * count + b * first_local, first_local), :] = values[
                :, j * third_length : (j + 1) * third_length
            ].reshape(space_size, first_local, third_length)
    own = jnp.concatenate([jnp.sum(total, axis=0, keepdims=True) for total in sums], 0)
    if not first:
        own = jnp.concatenate([sums_in[...], own], 0)
    if last:
        extra = send.shape[1] - image_count * count
        own = jnp.concatenate([own, jnp.zeros((extra - own.shape[0], third_length), jnp.float32)], 0)
        for d in range(space_size):
            send[d, pl.ds(image_count * count, extra), :] = own
    else:
        sums_out[...] = own


def turn_kernel(sizes, received, back_third, back_second, second_table, third_table, send, scratch, planes):
    fields, space_size, first_local, second_local, second_length, third_length = sizes

    def put(x, values):
        planes[x] = potential_of(values)

    leave_spectrum(sizes, received, back_third[...], back_second[...], scratch, put)
    entering = scratch.reshape(fields, first_local * second_length, third_length)
    enter_spectrum(sizes, lambda x: planes[x], second_table[...], third_table[...], entering, send)


def leave_kernel(sizes, rows, cell_count, received, back_third, back_second, images, spacing, scratch):
    fields, space_size, first_local, second_local, second_length, third_length = sizes

    def put(x, values):
        for j in range(fields):
            images[j, x] = values[:, j * third_length : (j + 1) * third_length]

    leave_spectrum(sizes, received, back_third[...], back_second[...], scratch, put)
    count = fields * second_local * first_local
    total = received[0, pl.ds(count, received.shape[1] - count), :]
    for s in range(1, space_size):
        total = total + received[s, pl.ds(count, received.shape[1] - count), :]
    spacing[...] = jnp.sum(total, axis=1, keepdims=True)[:rows] / cell_count


def call(kernel, outs, scratch, *args, smem=0):
    space = [pl.BlockSpec(memory_space=pltpu.SMEM if i < smem else pltpu.VMEM) for i in range(len(args))]
    return pl.pallas_call(
        kernel,
        out_shape=[jax.ShapeDtypeStruct(shape, jnp.float32) for shape in outs],
        in_specs=space,
        out_specs=[pl.BlockSpec(memory_space=pltpu.VMEM) for _ in outs],
        scratch_shapes=[pltpu.VMEM(shape, jnp.float32) for shape in scratch],
        compiler_params=pltpu.CompilerParams(vmem_limit_bytes=48 << 20),
    )(*args)


def exchange(values):
    return lax.all_to_all(values, "space", 0, 0, tiled=True)


def local_tiled(images, weights):
    image_count, first_local, second_length, third_length = images.shape
    space_size = lax.axis_size("space")
    first_length = first_local * space_size
    second_local = second_length // space_size
    cell_count = first_length * second_length * third_length
    first, second, third = basis(first_length), basis(second_length), basis(third_length)
    enter_first, leave_first = left_table(first), left_table(first.T)
    enter_second, leave_second = left_table(second), left_table(second.T)
    enter_third, leave_third = right_table(third.T), right_table(third)
    count = second_local * first_local
    sizes = (space_size, first_local, second_local, second_length, third_length)
    rows = ITERS * (image_count - 1)
    extra = -(-rows // 8) * 8
    plain = (space_size, image_count * count, third_length)
    held = (space_size * image_count * count, third_length)
    send = call(
        functools.partial(enter_kernel, (2 * image_count,) + sizes),
        [(space_size, 2 * image_count * count, third_length)],
        [(2 * image_count, first_local * second_length, third_length)],
        images, enter_second, enter_third,
    )[0]
    spectrum = sums = None
    for iteration in range(ITERS):
        received = exchange(send)
        last = iteration == ITERS - 1
        outs = [(space_size, image_count * count + (extra if last else 0), third_length)]
        if not last:
            outs.append((second_local, image_count, first_length, third_length))
            outs.append(((iteration + 1) * (image_count - 1), third_length))
        state = () if iteration == 0 else (spectrum, sums)
        send, *state = call(
            lambda *refs, first=iteration == 0, last=last: relax_kernel((image_count,) + sizes, first, last, refs),
            outs, [], weights, received, *state, enter_first, leave_first, smem=1,
        )
        received = exchange(send)
        if not last:
            spectrum, sums = state
            send = call(
                functools.partial(turn_kernel, (image_count,) + sizes),
                [plain], [held, (first_local, second_length, image_count * third_length)],
                received, leave_third, leave_second, enter_second, enter_third,
            )[0]
    concentration, spacing = call(
        functools.partial(leave_kernel, (image_count,) + sizes, rows, cell_count),
        [images.shape, (rows, 1)], [held],
        received, leave_third, leave_second,
    )
    return concentration, spacing.reshape(ITERS, image_count - 1)


def local_plain(images, weights):
    image_count, first_local, second_length, third_length = images.shape
    space_size = lax.axis_size("space")
    position = lax.axis_index("space")
    first_length = first_local * space_size
    second_local = second_length // space_size
    first = jnp.asarray(basis(first_length)).reshape(first_length, space_size, first_local)
    second = jnp.asarray(basis(second_length)).reshape(space_size, second_local, second_length)
    third = jnp.asarray(basis(third_length))
    local_rows = position * second_local + jnp.arange(second_local, dtype=jnp.int32)
    squares = (
        wave_squares(second_length, local_rows)[:, None, None]
        + wave_squares(first_length, jnp.arange(first_length, dtype=jnp.int32))[None, :, None]
        + wave_squares(third_length, jnp.arange(third_length, dtype=jnp.int32))[None, None, :]
    )
    damping = 1.0 / (1.0 + time_step * gradient_weight * squares * squares)
    coupling = time_step * squares * damping
    cell_count = first_length * second_length * third_length

    def forward(values):
        values = jnp.einsum("sby,fxyz->fxsbz", second, values, precision=high)
        values = jnp.einsum("fxsbz,kz->sfbxk", values, third, precision=high)
        values = lax.all_to_all(values, "space", 0, 0, tiled=True)
        return jnp.einsum("asx,sfbxk->fbak", first, values, precision=high)

    def backward(values, extra):
        values = jnp.einsum("asx,fbak->sfbxk", first, values, precision=high)
        sent = values.reshape(space_size, -1, third_length)
        if extra is not None:
            rows = jnp.broadcast_to(extra, (space_size,) + extra.shape)
            sent = jnp.concatenate([sent, rows], 1)
        sent = lax.all_to_all(sent, "space", 0, 0, tiled=True)
        count = values.size // (space_size * third_length)
        received = sent[:, :count].reshape(values.shape)
        values = jnp.einsum("sfbxk,kz->fxsbz", received, third, precision=high)
        values = jnp.einsum("sby,fxsbz->fxyz", second, values, precision=high)
        return values, sent[:, count:]

    concentration = images
    spectrum = None
    sums = []
    for iteration in range(ITERS):
        potential = concentration * concentration * concentration - concentration
        if iteration == 0:
            spectra = forward(jnp.concatenate([concentration, potential]))
            spectrum, potential = spectra[:image_count], spectra[image_count:]
        else:
            potential = forward(potential)
        spectrum = spectrum * damping - potential * coupling
        difference = spectrum[1:] - spectrum[:-1]
        sums.append(jnp.sum(difference * difference, axis=(1, 2, 3)))
        spectrum = jnp.einsum("ij,jbak->ibak", weights, spectrum, precision=lax.Precision.HIGHEST)
        extra = None
        if iteration == ITERS - 1:
            partial_sums = jnp.concatenate(sums)
            extra = jnp.pad(partial_sums[None], ((0, 7), (0, third_length - partial_sums.size)))
        concentration, extra = backward(spectrum, extra)
    totals = jnp.sum(extra[:, 0], axis=0)[: ITERS * (image_count - 1)] / cell_count
    return (concentration, totals.reshape(ITERS, image_count - 1))


def local(images, weights):
    first_local = images.shape[1]
    second_local = images.shape[2] // lax.axis_size("space")
    tiled = first_local % 8 == 0 and second_local % 8 == 0 and images.shape[3] % 128 == 0
    return (local_tiled if tiled else local_plain)(images, weights)


def solution(mesh):
    placed = (P("group", "space", None, None), P("group", None))
    return jax.shard_map(
        local,
        mesh=mesh,
        in_specs=placed,
        out_specs=(P("group", "space", None, None), P("group", None)),
        check_vma=False,
    )
```
